32 devices in a mesh: expert: 8 (over y, x, core), section: 4 (over z).
Axes of the slice: x: 2, y: 2, z: 4, core: 2. Of those that a mesh axis runs over, the one named last changes fastest.
Arguments:
- rows_in: bfloat16 [8, 512, 3072], P('expert', 'section'), may hold values from -6 to 6
- route_prob: float32 [8, 512], P('expert', 'section'), may hold values from 0.2 to 1
- w_in: bfloat16 [8, 128, 8, 3072], P('expert', 'section'), may hold values from -0.109375 to 0.109375
- w_down: bfloat16 [8, 128, 4, 3072], P('expert', 'section'), may hold values from -0.5 to 0.5
- m_send: float32 [8, 48, 3072], P('expert', 'section'), may hold values from -6 to 6
- v_send: float32 [8, 48, 3072], P('expert', 'section'), may hold values from 0.01 to 1
- chosen: int32 [8, 4], P('expert', 'section'), may hold values from 0 to 31
- swap_mask: int32 [4], P('section'), may hold values from 1 to 7, as said below
- dest_slot: int32 [8, 512], P('expert', 'section'), may hold values from 0 to 7, as said below
- dest_row: int32 [8, 512], P('expert', 'section'), may hold values from 0 to 191, as said below
Outputs:
- routed: bfloat16 [8, 768, 3072], P('expert', 'section')
- m_recv: float32 [8, 48, 3072], P('expert', 'section')
- v_recv: float32 [8, 48, 3072], P('expert', 'section')
The draws below stay inside these ranges and needn't reach their ends.
Inputs may be any that keep to these rules, and one draw needn't show every extreme that they name: `swap_mask`: the mask of one section sets every bit of a slot index. `dest_slot`: among the rows of one slot, at most 32 go to one slot of the next section, and one slot of the next section receives 192 rows in all; no slot receives more. `dest_row`: rows arriving at one slot of the next section have distinct destination rows.
All inputs are finite; a program needn't handle non-finite values.
Results may differ from the reference program's by a relative error of at most 0.0049.
Values may be sent and summed in bfloat16 or wider, within the bound.
No kernel may reach another device: no remote copies, remote signals or barrier semaphores. Data moves between devices by JAX's collectives and lax.ppermute only.
A program may use at most 64 MiB of HBM per device.

```python
import math
import jax
import jax.numpy as jnp
from jax import lax

D = 3072
ROWS_DEV = 128
PANELS = 32
PANEL_UNITS = 4
OUT_ROWS = 192
N_EXPERT = 8
N_SECTION = 4


def section_routes(key):
    peer_count = N_EXPERT
    row_count = ROWS_DEV
    out_rows = row_count + row_count // 2
    keys = jax.random.split(key, 5)
    hot_slot = jax.random.randint(keys[0], (), 0, peer_count).astype(jnp.int32)
    shuffled = jax.random.permutation(keys[1], peer_count)
    heavy_src = jnp.zeros((peer_count,), jnp.int32).at[shuffled[:peer_count // 2]].set(1)
    victim = (hot_slot + 1 + jax.random.randint(keys[2], (peer_count,), 0, peer_count - 1)) % peer_count
    sources = jnp.arange(peer_count, dtype=jnp.int32)[:, None]
    positions = jnp.arange(row_count, dtype=jnp.int32)[None, :]
    target = (sources + positions) % peer_count
    redirect = (heavy_src[:, None] == 1) & (target == victim[:, None].astype(jnp.int32))
    target = jnp.where(redirect, hot_slot, target).astype(jnp.int32)
    onehot = (target[:, :, None] == jnp.arange(peer_count, dtype=jnp.int32)[None, None, :]).astype(jnp.int32)
    counts = jnp.sum(onehot, 1)
    before = jnp.cumsum(counts, 0) - counts
    within = jnp.cumsum(onehot, 1) - onehot
    ranks = jnp.sum((before[:, None, :] + within) * onehot, 2).astype(jnp.int32)
    sigma = jax.vmap(lambda sub_key: jax.random.permutation(sub_key, out_rows))(jax.random.split(keys[3], peer_count))
    landing = sigma[target, ranks].astype(jnp.int32)
    order = jax.vmap(lambda sub_key: jax.random.permutation(sub_key, row_count))(jax.random.split(keys[4], peer_count))
    slot_table = jnp.zeros((peer_count, row_count), jnp.int32).at[sources, order].set(target)
    row_table = jnp.zeros((peer_count, row_count), jnp.int32).at[sources, order].set(landing)
    return (slot_table, row_table)


def routing_tables(key):
    keys = jax.random.split(jax.random.fold_in(key, 11), N_SECTION)
    slot_all, row_all = jax.vmap(section_routes)(keys)
    slot_all = jnp.transpose(slot_all, (1, 0, 2)).reshape(N_EXPERT, N_SECTION * ROWS_DEV)
    row_all = jnp.transpose(row_all, (1, 0, 2)).reshape(N_EXPERT, N_SECTION * ROWS_DEV)
    return (slot_all, row_all)


def draw_dest_slot(key, part):
    return routing_tables(key)[0]


def draw_dest_row(key, part):
    return routing_tables(key)[1]


def draw_swap_mask(key, part):
    masks = jax.random.randint(jax.random.fold_in(key, 3), (N_SECTION,), 1, N_EXPERT).astype(jnp.int32)
    which = jax.random.randint(jax.random.fold_in(key, 5), (), 0, N_SECTION)
    return masks.at[which].set(N_EXPERT - 1).astype(jnp.int32)


def set_ends(values, own_key, low, largest):
    place = [jax.random.randint(jax.random.fold_in(own_key, axis), (), 0, length) for axis, length in enumerate(values.shape)]
    main_axis = values.shape.index(max(values.shape))
    neighbour = place[:main_axis] + [(place[main_axis] + 1) % values.shape[main_axis]] + place[main_axis + 1:]
    return values.at[tuple(place)].set(low).at[tuple(neighbour)].set(largest)


def shard_levels(own_key, extent, cuts, least, high):
    level, own = 1.0, jax.random.fold_in(own_key, 6)
    for position, shards_of in cuts:
        draws = jnp.exp(jax.random.uniform(jax.random.fold_in(own, position), (shards_of,), jnp.float32, least / len(cuts), high / len(cuts)))
        level = level * jnp.repeat(draws, extent[position] // shards_of).reshape([-1 if axis == position else 1 for axis in range(len(extent))])
    return level


def gaussian(rng, extent, spread, reach, cuts=(), held_as=jnp.bfloat16):
    drawn = spread * jax.random.normal(rng, extent, jnp.float32)
    if cuts:
        drawn = drawn * shard_levels(rng, extent, cuts, -0.22, 0.18)
    return jnp.clip(drawn, -reach, reach).astype(held_as)


def setup_inputs(seed: int = 0) -> dict:
    seeds = jax.random.split(jax.random.key(seed), 11)
    rows_in = gaussian(seeds[0], (N_EXPERT, N_SECTION * ROWS_DEV, D), 1.0, 6.0, ((0, 8), (1, 4)))
    route_prob = jnp.clip(0.2 + 0.8 * jax.random.uniform(seeds[1], (N_EXPERT, N_SECTION * ROWS_DEV), jnp.float32) ** shard_levels(seeds[1], (N_EXPERT, N_SECTION * ROWS_DEV), ((0, 8), (1, 4)), -0.2, 0.2), 0.2, 1.0)
    w_in = gaussian(seeds[2], (N_EXPERT, N_SECTION * PANELS, 2 * PANEL_UNITS, D), D ** -0.5, 0.109375, ((0, 8), (1, 4)))
    w_down = gaussian(seeds[3], (N_EXPERT, N_SECTION * PANELS, PANEL_UNITS, D), (PANELS * PANEL_UNITS) ** -0.5, 0.5, ((0, 8), (1, 4)))
    m_send = gaussian(seeds[4], (N_EXPERT, N_SECTION * 3 * PANEL_UNITS, D), 1.0, 6.0, ((0, 8), (1, 4)), jnp.float32)
    v_send = jnp.clip(jnp.exp(math.log(1.0) - 4.6051702 * jax.random.uniform(seeds[5], (N_EXPERT, N_SECTION * 3 * PANEL_UNITS, D), jnp.float32) ** shard_levels(seeds[5], (N_EXPERT, N_SECTION * 3 * PANEL_UNITS, D), ((0, 8), (1, 4)), -0.2, 0.2)), 0.01, 1.0)
    chosen = set_ends(jax.random.randint(seeds[6], (N_EXPERT, N_SECTION), 0, PANELS), jax.random.fold_in(seeds[6], 1), 0, PANELS - 1).astype(jnp.int32)
    swap_mask = draw_swap_mask(jax.random.fold_in(seeds[10], 71), 0)
    dest_slot = draw_dest_slot(jax.random.fold_in(seeds[10], 71), 0)
    dest_row = draw_dest_row(jax.random.fold_in(seeds[10], 71), 0)
    return {"rows_in": rows_in, "route_prob": route_prob, "w_in": w_in, "w_down": w_down, "m_send": m_send, "v_send": v_send, "chosen": chosen, "swap_mask": swap_mask, "dest_slot": dest_slot, "dest_row": dest_row}


def expert_block(operands):
    tokens, weight_in, weight_down, scales = operands
    gate_w = weight_in[:, :PANEL_UNITS].reshape(PANELS * PANEL_UNITS, D)
    up_w = weight_in[:, PANEL_UNITS:].reshape(PANELS * PANEL_UNITS, D)
    down_w = weight_down.reshape(PANELS * PANEL_UNITS, D)
    gate_pre = jnp.dot(tokens, gate_w.T, preferred_element_type=jnp.float32)
    up_pre = jnp.dot(tokens, up_w.T, preferred_element_type=jnp.float32)
    hidden = (jax.nn.silu(gate_pre) * up_pre).astype(jnp.bfloat16)
    mixed = jnp.dot(hidden, down_w, preferred_element_type=jnp.float32)
    return (scales[:, None] * mixed).astype(jnp.bfloat16)


def reference(rows_in, route_prob, w_in, w_down, m_send, v_send, chosen, swap_mask, dest_slot, dest_row):
    experts = jnp.arange(N_EXPERT, dtype=jnp.int32)
    panel_in = w_in.reshape(N_EXPERT, N_SECTION, PANELS, 2 * PANEL_UNITS, D)
    panel_down = w_down.reshape(N_EXPERT, N_SECTION, PANELS, PANEL_UNITS, D)
    first = m_send.reshape(N_EXPERT, N_SECTION, 3 * PANEL_UNITS, D)
    second = v_send.reshape(N_EXPERT, N_SECTION, 3 * PANEL_UNITS, D)
    routed = jnp.zeros((N_EXPERT * N_SECTION * OUT_ROWS, D), jnp.bfloat16)
    first_out = []
    second_out = []
    for section in range(N_SECTION):
        partner = jnp.bitwise_xor(experts, swap_mask[section]).astype(jnp.int32)
        own_pick = chosen[:, section].astype(jnp.int32)
        given_panel = own_pick[partner]
        arrive_in = panel_in[partner, section, given_panel]
        arrive_down = panel_down[partner, section, given_panel]
        slot_hit = (jnp.arange(PANELS, dtype=jnp.int32)[None, :] == own_pick[:, None])[:, :, None, None]
        new_in = jnp.where(slot_hit, arrive_in[:, None], panel_in[:, section])
        new_down = jnp.where(slot_hit, arrive_down[:, None], panel_down[:, section])
        first_out.append(first[partner, section])
        second_out.append(second[partner, section])
        tokens = rows_in[:, section * ROWS_DEV:(section + 1) * ROWS_DEV]
        scales = route_prob[:, section * ROWS_DEV:(section + 1) * ROWS_DEV]
        expert_rows = lax.map(expert_block, (tokens, new_in, new_down, scales))
        slot_ids = dest_slot[:, section * ROWS_DEV:(section + 1) * ROWS_DEV].astype(jnp.int32)
        places = dest_row[:, section * ROWS_DEV:(section + 1) * ROWS_DEV].astype(jnp.int32)
        following = (section + 1) % N_SECTION
        flat_index = (slot_ids * N_SECTION + following) * OUT_ROWS + places
        routed = routed.at[flat_index.reshape(-1)].set(expert_rows.reshape(-1, D))
    m_recv = jnp.stack(first_out, 1).reshape(N_EXPERT, N_SECTION * 3 * PANEL_UNITS, D)
    v_recv = jnp.stack(second_out, 1).reshape(N_EXPERT, N_SECTION * 3 * PANEL_UNITS, D)
    return routed.reshape(N_EXPERT, N_SECTION * OUT_ROWS, D), m_recv, v_recv
```

```python
import functools

import jax
import jax.numpy as jnp
from jax import lax
from jax.experimental import pallas as pl
from jax.experimental.pallas import tpu as pltpu
from jax.sharding import PartitionSpec as P

BF16 = jnp.bfloat16
F32 = jnp.float32
I32 = jnp.int32
LANES = 128
WIDTHS = (1536, 1536)
INFO = 16


def xor_permute(x, mask):
    return lax.ppermute(x, "expert", [(i, i ^ mask) for i in range(lax.axis_size("expert"))])


def next_section(x):
    n = lax.axis_size("section")
    return lax.ppermute(x, "section", [(i, (i + 1) % n) for i in range(n)])


def swap_with_partner(arrays, pair_mask):
    levels = lax.axis_size("expert").bit_length() - 1
    for low in range(0, levels, 3):
        count = min(3, levels - low)
        digit = jnp.bitwise_and(jnp.right_shift(pair_mask, low), (1 << count) - 1)

        def branch(value, low=low):
            if value == 0:
                return lambda xs: xs
            return lambda xs: tuple(xor_permute(x, value << low) for x in xs)

        if levels <= 3:
            arrays = lax.switch(digit - 1, [branch(v) for v in range(1, 1 << count)], arrays)
        else:
            arrays = lax.switch(digit, [branch(v) for v in range(1 << count)], arrays)
    return arrays


def vmem(n):
    return [pl.BlockSpec(memory_space=pltpu.VMEM)] * n


def panel_kernel(chosen_ref, w_in_ref, w_down_ref, out_ref):
    units = w_down_ref.shape[1]
    out_ref[0 : 2 * units, :] = w_in_ref[0]
    out_ref[2 * units : 3 * units, :] = w_down_ref[0]
    out_ref[3 * units : 4 * units, :] = w_down_ref[0]


def take_panel(chosen, w_in, w_down):
    _, units, width = w_down.shape
    grid_spec = pltpu.PrefetchScalarGridSpec(
        num_scalar_prefetch=1,
        grid=(1,),
        in_specs=[
            pl.BlockSpec((1, 2 * units, width), lambda i, c: (c[0], 0, 0)),
            pl.BlockSpec((1, units, width), lambda i, c: (c[0], 0, 0)),
        ],
        out_specs=pl.BlockSpec((4 * units, width), lambda i, c: (0, 0)),
    )
    return pl.pallas_call(
        panel_kernel,
        grid_spec=grid_spec,
        out_shape=jax.ShapeDtypeStruct((4 * units, width), BF16),
        name="take_panel",
    )(chosen, w_in, w_down)


def dot_t(a, b):
    return lax.dot_general(a, b, (((1,), (1,)), ((), ())), preferred_element_type=F32)


def dot(a, b):
    return jnp.dot(a, b, preferred_element_type=F32)


def gated(pre):
    lanes = pre.shape[1]
    return (jax.nn.silu(pre) * pltpu.roll(pre, lanes - 4, 1)).astype(BF16)


def hidden_kernel(chosen_ref, tok_ref, w_ref, new_ref, prob_ref, slot_ref, row_ref, out_ref, pad_ref, down_ref):
    rows, width = tok_ref.shape
    units = 4
    chosen = chosen_ref[0]
    tokens = tok_ref[...]
    pad_ref[...] = jnp.zeros_like(pad_ref)
    pad_ref[0 : 4 * units, :] = new_ref[...]
    own = gated(dot_t(tokens, w_ref[...]))
    new = gated(dot_t(tokens, pad_ref[...]))
    col = lax.broadcasted_iota(I32, (2 * rows, rows), 0)
    unit = lax.broadcasted_iota(I32, (2 * rows, rows), 1)
    keep = ((col >> 3) == (unit >> 2)) & ((col & 7) == (unit & 3)) & ((unit >> 2) != chosen)
    col2 = lax.broadcasted_iota(I32, (LANES, rows), 0)
    unit2 = lax.broadcasted_iota(I32, (LANES, rows), 1)
    put = (col2 == (unit2 & 3)) & ((unit2 >> 2) == chosen)
    hidden = dot(own, keep.astype(F32).astype(BF16)) + dot(new, put.astype(F32).astype(BF16))
    out_ref[0:rows, :] = hidden.astype(BF16)

    i0 = lax.broadcasted_iota(I32, (rows, rows), 0)
    i1 = lax.broadcasted_iota(I32, (rows, rows), 1)
    slot = slot_ref[...].astype(F32)
    slot_col = jnp.sum(jnp.where(i0 == i1, slot, 0.0), axis=1, keepdims=True)
    rank = jnp.sum(jnp.where((slot_col == slot) & (i0 < i1), 1.0, 0.0), axis=0, keepdims=True)
    prob = prob_ref[...]
    p0 = prob.astype(BF16).astype(F32)
    p1 = (prob - p0).astype(BF16).astype(F32)
    p2 = prob - p0 - p1
    fields = (slot, rank, row_ref[...].astype(F32), p0, p1, p2, jnp.full((1, rows), chosen, I32).astype(F32))
    line = lax.broadcasted_iota(I32, (INFO, rows), 0)
    info = jnp.zeros((INFO, rows), F32)
    for number, field in enumerate(fields):
        info = jnp.where(line == number, field, info)
    out_ref[rows : rows + INFO, :] = info.astype(BF16)

    down = new_ref[2 * units : 4 * units, :].astype(F32)
    for t in range(width // LANES):
        down_ref[units * t : units * (t + 1), :] = down[0:units, LANES * t : LANES * (t + 1)]
    out_ref[rows + INFO :, :] = down_ref[...].astype(BF16)


def make_hidden(chosen, tokens, w_in, new_panel, prob, slot, row):
    rows, width = tokens.shape
    extra = 4 * (width // LANES)
    return pl.pallas_call(
        hidden_kernel,
        in_specs=[pl.BlockSpec(memory_space=pltpu.SMEM)] + vmem(6),
        out_specs=pl.BlockSpec(memory_space=pltpu.VMEM),
        out_shape=jax.ShapeDtypeStruct((rows + INFO + extra, rows), BF16),
        scratch_shapes=[pltpu.VMEM((LANES, width), BF16), pltpu.VMEM((extra, LANES), F32)],
        cost_estimate=pl.CostEstimate(flops=3 * 2 * rows * rows * width, bytes_accessed=2500000, transcendentals=0),
        name="make_hidden",
    )(chosen, tokens, w_in, new_panel, prob, slot, row)


def rows_kernel(start, width, labelled, me_ref, ha_ref, hb_ref, da_ref, db_ref, *refs):
    outs, down_ref = refs[:-1], refs[-1]
    rows = LANES
    chips = len(outs)
    cap = rows // chips
    chip, core = me_ref[0] >> 1, me_ref[0] & 1
    i0 = lax.broadcasted_iota(I32, (rows, rows), 0)
    for src, (h_ref, d_ref) in enumerate(((ha_ref, da_ref), (hb_ref, db_ref))):
        info = h_ref[rows : rows + INFO, :].astype(F32)
        slot = info[0:1].astype(I32)
        rank = info[1:2].astype(I32)
        prob = info[3:4] + info[4:5] + info[5:6]
        block = jnp.bitwise_xor(slot >> 1, chip)
        place = jnp.where((slot & 1) == core, block * cap + rank, -1)
        hit = i0 == place
        packed = dot(hit.astype(F32).astype(BF16), h_ref[0:rows, :]).astype(BF16)
        scale = jnp.sum(jnp.where(hit, prob, 0.0), axis=1, keepdims=True)
        replaced = (i0 >> 2) == info[6:7].astype(I32)
        down_ref[...] = h_ref[rows + INFO :, :].astype(F32)
        for t in range(width // LANES):
            four = down_ref[4 * (start // LANES + t) : 4 * (start // LANES + t) + 4, :]
            eight = jnp.concatenate([four, four], axis=0)
            tiled = jnp.broadcast_to(eight[None], (rows // 8, 8, LANES)).reshape(rows, LANES)
            cols = slice(LANES * t, LANES * (t + 1))
            down = jnp.where(replaced, tiled, d_ref[:, cols].astype(F32)).astype(BF16)
            value = (scale * dot(packed, down)).astype(BF16)
            for k in range(chips):
                outs[k][src * cap : (src + 1) * cap, cols] = value[k * cap : (k + 1) * cap]
        if labelled:
            label = jnp.sum(jnp.where(hit, info[2:3] + 1.0, 0.0), axis=1, keepdims=True) - 1.0
            label = jnp.broadcast_to(label, (rows, LANES)).astype(BF16)
            for k in range(chips):
                outs[k][src * cap : (src + 1) * cap, width:] = label[k * cap : (k + 1) * cap]


def make_rows(me, ha, hb, da, db, start, labelled):
    width = da.shape[1]
    chips = lax.axis_size("expert") // 2
    out_width = width + LANES * labelled
    extra = ha.shape[0] - LANES - INFO
    return pl.pallas_call(
        functools.partial(rows_kernel, start, width, labelled),
        in_specs=[pl.BlockSpec(memory_space=pltpu.SMEM)] + vmem(4),
        out_specs=vmem(chips),
        out_shape=[jax.ShapeDtypeStruct((2 * LANES // chips, out_width), BF16)] * chips,
        scratch_shapes=[pltpu.VMEM((extra, LANES), F32)],
        cost_estimate=pl.CostEstimate(flops=4 * LANES * LANES * width, bytes_accessed=8 * LANES * width, transcendentals=0),
        name="make_rows",
    )(me, ha, hb, da, db)


def place_kernel(chips, *refs):
    labels, data, out_ref = refs[:chips], refs[chips : 2 * chips], refs[-1]
    count = labels[0].shape[0]
    i0 = lax.broadcasted_iota(I32, (count, LANES), 0)
    i1 = lax.broadcasted_iota(I32, (count, LANES), 1)
    spread = [jnp.sum(jnp.where(i0 == i1, ref[...].astype(F32), 0.0), axis=0, keepdims=True) for ref in labels]
    label = jnp.concatenate([row[:, :count] for row in spread], axis=1)
    target = lax.broadcasted_iota(I32, (out_ref.shape[0], chips * count), 0)
    hit = (target == label.astype(I32)).astype(F32).astype(BF16)
    arrived = jnp.concatenate([ref[...] for ref in data], axis=0)
    out_ref[...] = dot(hit, arrived).astype(BF16)


def place_rows(labelled, data, buffer, start, out_rows, model_width):
    chips = len(data)
    count, width = data[0].shape
    label_at = labelled[0].shape[1] // LANES - 1
    if data[0] is labelled[0]:
        width -= LANES
    block = 512
    first = start // block
    operands = list(labelled) + list(data)
    in_specs = [pl.BlockSpec((count, LANES), lambda i: (0, label_at))] * chips
    in_specs += [pl.BlockSpec((count, block), lambda i: (0, i))] * chips
    aliases = {}
    if buffer is not None:
        operands.append(buffer)
        in_specs.append(pl.BlockSpec(memory_space=pl.ANY))
        aliases = {2 * chips: 0}
    return pl.pallas_call(
        functools.partial(place_kernel, chips),
        grid=(width // block,),
        in_specs=in_specs,
        out_specs=pl.BlockSpec((out_rows, block), lambda i: (0, first + i)),
        out_shape=jax.ShapeDtypeStruct((out_rows, model_width), BF16),
        input_output_aliases=aliases,
        cost_estimate=pl.CostEstimate(flops=2 * out_rows * 2 * LANES * width, bytes_accessed=1000 * width, transcendentals=0),
        name="place_rows",
    )(*operands)


def per_device_chips(
    rows_in, route_prob, w_in, w_down, m_send, v_send, chosen, swap_mask, dest_slot, dest_row
):
    panels, units, model_width = w_down.shape[1:]
    slots = lax.axis_size("expert")
    chips = slots // 2
    rows = rows_in.shape[1]
    out_rows = rows + rows // 2
    me = lax.axis_index("expert").astype(I32).reshape(1)
    starts = [sum(WIDTHS[:i]) for i in range(len(WIDTHS))]

    down = w_down[0].reshape(panels * units, model_width)
    own_down = [next_section(down[:, s : s + w]) for s, w in zip(starts, WIDTHS)]

    panel = take_panel(chosen.reshape(1), w_in[0], w_down[0])
    moments = jnp.concatenate([m_send[0], v_send[0]], 0).astype(BF16)
    panel, moments = swap_with_partner((panel, moments), swap_mask[0])
    w_flat = w_in[0].reshape(panels * 2 * units, model_width)
    hidden = make_hidden(chosen.reshape(1), rows_in[0], w_flat, panel, route_prob, dest_slot, dest_row)
    hidden = next_section(hidden)
    side_hidden = xor_permute(hidden, 1)
    side_down = [xor_permute(d, 1) for d in own_down]

    labelled, buffer = None, None
    for i, (start, width) in enumerate(zip(starts, WIDTHS)):
        made = make_rows(me, hidden, side_hidden, own_down[i], side_down[i], start, i == 0)
        data = [made[0]] + [xor_permute(made[k], 2 * k) for k in range(1, chips)]
        if labelled is None:
            labelled = data
        buffer = place_rows(labelled, data, buffer, start, out_rows, model_width)
    half = m_send.shape[1]
    moments = moments.astype(F32)
    return (buffer[None], moments[:half][None], moments[half:][None])


def from_partner(x, axis, apart):
    return lax.ppermute(x, axis, [(i, i ^ 1 << apart) for i in range(lax.axis_size(axis))])


def scatter_rows(arrived_rows, arrived_labels, out_rows):
    model_width = arrived_rows.shape[-1]
    buffer = jnp.zeros((out_rows, model_width), BF16)
    return buffer.at[arrived_labels.reshape(-1)].set(
        arrived_rows.reshape(-1, model_width), mode="drop"
    )


def pack_rows(expert_rows, target, landing, peer_count, capacity, out_rows):
    model_width = expert_rows.shape[-1]
    onehot = (target[:, None] == jnp.arange(peer_count, dtype=I32)[None, :]).astype(I32)
    position = jnp.sum((jnp.cumsum(onehot, 0) - onehot) * onehot, 1)
    packed = jnp.zeros((peer_count, capacity, model_width), BF16)
    packed = packed.at[target, position].set(expert_rows)
    labels = jnp.full((peer_count, capacity), out_rows, I32).at[target, position].set(landing)
    return (packed, labels)


def per_device_general(
    rows_in, route_prob, w_in, w_down, m_send, v_send, chosen, swap_mask, dest_slot, dest_row
):
    panels, units, model_width = w_down.shape[1:]
    given_in = lax.dynamic_index_in_dim(w_in[0], chosen[0, 0], 0, keepdims=False)
    given_down = lax.dynamic_index_in_dim(w_down[0], chosen[0, 0], 0, keepdims=False)
    weights = jnp.concatenate([given_in, given_down], 0)
    moments = jnp.stack([m_send[0], v_send[0]], 0)
    for bit in range(lax.axis_size("expert").bit_length() - 1):
        arrived_w = from_partner(weights, "expert", bit)
        arrived_m = from_partner(moments, "expert", bit)
        flag = jnp.bitwise_and(jnp.right_shift(swap_mask[0], bit), 1) == 1
        weights = jnp.where(flag, arrived_w, weights)
        moments = jnp.where(flag, arrived_m, moments)
    slot_hit = (jnp.arange(panels, dtype=I32) == chosen[0, 0])[:, None, None]
    new_in = jnp.where(slot_hit, weights[None, : 2 * units], w_in[0])
    new_down = jnp.where(slot_hit, weights[None, 2 * units :], w_down[0])
    gate_w = new_in[:, :units].reshape(panels * units, model_width)
    up_w = new_in[:, units:].reshape(panels * units, model_width)
    down_w = new_down.reshape(panels * units, model_width)
    tokens = rows_in[0]
    hidden = (jax.nn.silu(dot_t(tokens, gate_w)) * dot_t(tokens, up_w)).astype(BF16)
    expert_rows = (route_prob[0][:, None] * dot(hidden, down_w)).astype(BF16)
    peers = lax.axis_size("expert")
    rows = tokens.shape[0]
    capacity = 2 * rows // peers
    out_rows = rows + rows // 2
    moved = next_section((expert_rows, dest_slot[0], dest_row[0]))
    packed, labels = pack_rows(*moved, peers, capacity, out_rows)
    packed = lax.all_to_all(packed, "expert", split_axis=0, concat_axis=0, tiled=True)
    labels = lax.all_to_all(labels, "expert", split_axis=0, concat_axis=0, tiled=True)
    routed = scatter_rows(packed, labels, out_rows)
    return (routed[None], moments[0][None], moments[1][None])


def solution(mesh):
    plane = P("expert", "section", None)
    line = P("expert", "section")
    block = P("expert", "section", None, None)
    in_specs = (plane, line, block, block, plane, plane, line, P("section"), line, line)
    few = mesh.shape["expert"] == 8
    return jax.shard_map(
        per_device_chips if few else per_device_general,
        mesh=mesh,
        in_specs=in_specs,
        out_specs=(plane, plane, plane),
        check_vma=False,
    )
```
